32 devices in a mesh: ra: 4 (over x, core), rb: 8 (over z, y).
Axes of the slice: x: 2, y: 2, z: 4, core: 2. Of those that a mesh axis runs over, the one named last changes fastest.
Arguments:
- features_a: bfloat16 [8, 128, 1024], P('ra', 'rb'), may hold values from -600 to 600
- features_b: bfloat16 [16, 128, 1024], P('rb', 'ra'), may hold values from -600 to 600
- weight_one: bfloat16 [16, 81], replicated, may hold values from -16 to 16
- bias_one: float32 [16], replicated, may hold values from -3 to 3
- weight_two: bfloat16 [16, 81], replicated, may hold values from -0.25 to 0.25
- bias_two: float32 [1], replicated, may hold values from -3 to 3
Outputs:
- consensus: float32 [8, 128, 16, 128], P('ra', None, 'rb')
The draws below stay inside these ranges and needn't reach their ends.
All inputs are finite; a program needn't handle non-finite values.
Results may differ from the reference program's by a relative error of at most 0.0053.
Values may be sent and summed in bfloat16 or wider, within the bound.
No kernel may reach another device: no remote copies, remote signals or barrier semaphores. Data moves between devices by JAX's collectives and lax.ppermute only.
A program may use at most 192 MiB of HBM per device.

```python
import math
import jax
import jax.numpy as jnp
from jax import lax

C = 1024
HID = 16
W = 128
HA = 8
HB = 16


def draw_grid(key, rows):
    key_noise, key_cell, key_chan = jax.random.split(key, 3)
    noise = jax.random.truncated_normal(key_noise, -5.0, 5.0, (rows, W, C), jnp.float32)
    channel = jnp.exp(jax.random.uniform(key_chan, (C,), jnp.float32, 0.0, math.log(10.0)))
    cell_scale = jnp.exp(jax.random.uniform(key_cell, (rows, W, 1), jnp.float32, 0.0, math.log(10.0)))
    return noise * cell_scale * channel


def draw_features_a(key, part):
    return draw_grid(jax.random.fold_in(key, 11), HA).astype(jnp.bfloat16)


def draw_features_b(key, part):
    return draw_grid(jax.random.fold_in(key, 23), HB).astype(jnp.bfloat16)


def gaussian(rng, dims, spread, bound, kind=jnp.bfloat16):
    array = jax.random.normal(rng, dims, jnp.float32) * spread
    return jnp.minimum(jnp.maximum(array, -bound), bound).astype(kind)


def setup_inputs(seed: int = 0) -> dict:
    arg_keys = jax.random.split(jax.random.key(seed), 7)
    return {
        "features_a": draw_features_a(jax.random.fold_in(arg_keys[6], 71), 0),
        "features_b": draw_features_b(jax.random.fold_in(arg_keys[6], 71), 0),
        "weight_one": gaussian(arg_keys[2], (HID, 81), 2.5, 16.0),
        "bias_one": gaussian(arg_keys[3], (HID,), 0.5, 3.0, jnp.float32),
        "weight_two": gaussian(arg_keys[4], (HID, 81), (HID * 40) ** -0.5, 0.25),
        "bias_two": gaussian(arg_keys[5], (1,), 0.5, 3.0, jnp.float32),
    }


def normalize(features):
    values = features.astype(jnp.float32)
    scale = lax.rsqrt(lax.optimization_barrier(jnp.sum(values * values, axis=-1, keepdims=True)) + 1e-06)
    return (values * scale).astype(jnp.bfloat16)

def first_layer(volume, weight_one, bias_one, out_rows, out_k):
    width_j = volume.shape[1] - 2
    width_l = volume.shape[3] - 2
    weights = weight_one.astype(jnp.float32)

    def one_row(row_start):
        block = lax.dynamic_slice_in_dim(volume, row_start, 3, 0)
        patches = jnp.stack([block[t_i, t_j:t_j + width_j, t_k:t_k + out_k, t_l:t_l + width_l] for t_i in range(3) for t_j in range(3) for t_k in range(3) for t_l in range(3)])
        before = lax.dot_general(weights, patches.astype(jnp.float32), (((1,), (0,)), ((), ())))
        return jax.nn.relu(before + bias_one[:, None, None, None])
    return lax.map(one_row, jnp.arange(out_rows, dtype=jnp.int32))

def second_layer(hidden_pad, weight_two, bias_two, out_rows, out_k):
    width_j = hidden_pad.shape[2] - 2
    width_l = hidden_pad.shape[4] - 2
    weights = weight_two.astype(jnp.float32)

    def one_row(row_start):
        total = jnp.zeros((width_j, out_k, width_l), jnp.float32)
        for t_i in range(3):
            plane = lax.dynamic_index_in_dim(hidden_pad, row_start + t_i, 0, keepdims=False)
            taps = lax.dot_general(weights[:, 27 * t_i:27 * t_i + 27], plane.astype(jnp.float32), (((0,), (0,)), ((), ())))
            for t_j in range(3):
                for t_k in range(3):
                    for t_l in range(3):
                        total = total + taps[9 * t_j + 3 * t_k + t_l, t_j:t_j + width_j, t_k:t_k + out_k, t_l:t_l + width_l]
        return jax.nn.relu(total + bias_two[0])
    return lax.map(one_row, jnp.arange(out_rows, dtype=jnp.int32))

def reference(features_a, features_b, weight_one, bias_one, weight_two, bias_two):
    norm_a = normalize(features_a)
    norm_b = normalize(features_b)
    rows_a, width_j, channels = norm_a.shape
    rows_b, width_l, _ = norm_b.shape
    corr = jnp.dot(norm_a.reshape(-1, channels), norm_b.reshape(-1, channels).T, preferred_element_type=jnp.float32)
    corr = corr.reshape(rows_a, width_j, rows_b, width_l).astype(jnp.bfloat16)
    padded = jnp.pad(corr, 1)
    hidden = first_layer(padded, weight_one, bias_one, rows_a, rows_b).astype(jnp.bfloat16)
    hidden_pad = jnp.pad(hidden, ((1, 1), (0, 0), (1, 1), (1, 1), (1, 1)))
    return second_layer(hidden_pad, weight_two, bias_two, rows_a, rows_b)
```

```python
import functools

import jax
import jax.numpy as jnp
import numpy as np
from jax import lax
from jax.experimental import pallas as pl
from jax.experimental.pallas import tpu as pltpu
from jax.sharding import PartitionSpec as P


WIN = 16
STEP = WIN - 2
VMEM = pltpu.VMEM
SMEM = pltpu.SMEM


def spread(block, axis):
    count = lax.axis_size(axis)
    return [block] + [
        lax.ppermute(block, axis, [(i, (i + s) % count) for i in range(count)])
        for s in range(1, count)
    ]


def halo(block, axis):
    count = lax.axis_size(axis)
    before = lax.ppermute(block, axis, [(i, i + 1) for i in range(count - 1)])
    after = lax.ppermute(block, axis, [(i + 1, i) for i in range(count - 1)])
    return before, after


def corr_kernel(n_a, n_b, place, *refs):
    a_refs = refs[:n_a]
    b_refs = refs[n_a : n_a + n_b]
    out, all_a, all_b = refs[n_a + n_b :]
    for pos, count, blocks, whole in ((1, n_a, a_refs, all_a), (0, n_b, b_refs, all_b)):
        for s, ref in enumerate(blocks):
            source = lax.rem(place[pos] - s + count, count)
            values = ref[...].astype(jnp.float32)
            scale = lax.rsqrt(jnp.sum(values * values, axis=-1, keepdims=True) + 1e-06)
            normed = (values * scale).astype(jnp.bfloat16)
            cols = ref.shape[1]
            whole[:, pl.ds(pl.multiple_of(source * cols, cols), cols), :] = normed.astype(whole.dtype)
    for k in range(out.shape[0]):
        row_b = all_b[k].astype(jnp.bfloat16)
        for i in range(out.shape[1]):
            out[k, i] = lax.dot_general(
                all_a[i].astype(jnp.bfloat16),
                row_b,
                (((1,), (1,)), ((), ())),
                preferred_element_type=jnp.float32,
            ).astype(jnp.bfloat16)


def correlate(place, blocks_a, blocks_b):
    rows_a, cols_a, channels = blocks_a[0].shape
    rows_b, cols_b, _ = blocks_b[0].shape
    wide_a, wide_b = cols_a * len(blocks_a), cols_b * len(blocks_b)
    kind_a = jnp.bfloat16 if cols_a % 16 == 0 else jnp.float32
    kind_b = jnp.bfloat16 if cols_b % 16 == 0 else jnp.float32
    return pl.pallas_call(
        functools.partial(corr_kernel, len(blocks_a), len(blocks_b)),
        out_shape=jax.ShapeDtypeStruct((rows_b, rows_a, wide_a, wide_b), jnp.bfloat16),
        in_specs=[pl.BlockSpec(memory_space=SMEM)]
        + [pl.BlockSpec(memory_space=VMEM)] * (len(blocks_a) + len(blocks_b)),
        out_specs=pl.BlockSpec(memory_space=VMEM),
        scratch_shapes=[
            VMEM((rows_a, wide_a, channels), kind_a),
            VMEM((rows_b, wide_b, channels), kind_b),
        ],
        name="correlate",
    )(place, *blocks_a, *blocks_b)


def band_tables(hid):
    taps = np.arange(81)
    ta, tb, tc, td = taps // 27, taps // 9 % 3, taps // 3 % 3, taps % 3
    col = np.arange(27 * WIN)
    ca, cc, cd, cw = col // (9 * WIN), col // (3 * WIN) % 3, col // WIN % 3, col % WIN
    pick = np.zeros((3, 81, 27 * WIN), np.float32)
    for b in range(3):
        pick[b] = (
            (tb[:, None] == b)
            & (ta[:, None] == ca[None])
            & (tc[:, None] == cc[None])
            & (td[:, None] == cd[None])
        )
    row = np.arange(hid * STEP)
    ro, rj = row // STEP, row % STEP
    grow = (ro[:, None] == np.arange(hid)[None]).astype(np.float32)
    return pick, grow, cw, rj


def band_kernel(pick, grow, w1, w2, bias, tail, band1, band2, bias_full):
    rows, cols = band1.shape
    jj = lax.broadcasted_iota(jnp.int32, (rows, cols), 0) % STEP
    ww = lax.broadcasted_iota(jnp.int32, (rows, cols), 1) % WIN
    total = jnp.zeros((rows, cols), jnp.float32)
    for b in range(3):
        wide = jnp.dot(w1[...], pick[b], preferred_element_type=jnp.float32).astype(jnp.bfloat16)
        tall = jnp.dot(grow[...], wide, preferred_element_type=jnp.float32)
        total = total + jnp.where(ww - jj == b, tall, 0.0)
    band1[...] = total.astype(jnp.bfloat16)
    jj = lax.broadcasted_iota(jnp.int32, (cols, rows), 1) % STEP
    rr = lax.broadcasted_iota(jnp.int32, (cols, rows), 0) % WIN
    total = jnp.zeros((cols, rows), jnp.float32)
    for b in range(3):
        wide = lax.dot_general(
            pick[b], w2[...], (((0,), (1,)), ((), ())), preferred_element_type=jnp.float32
        ).astype(jnp.bfloat16)
        tall = lax.dot_general(
            wide, grow[...], (((1,), (1,)), ((), ())), preferred_element_type=jnp.float32
        )
        total = total + jnp.where(jj - rr + 2 == b, tall, 0.0)
    band2[0] = total.astype(jnp.bfloat16)
    band2[1] = jnp.where(jj < tail, total, 0.0).astype(jnp.bfloat16)
    bias_full[...] = jnp.broadcast_to(
        lax.dot_general(
            grow[...].astype(jnp.float32),
            bias[...],
            (((1,), (0,)), ((), ())),
            precision=lax.Precision.HIGHEST,
            preferred_element_type=jnp.float32,
        ),
        bias_full.shape,
    )


def bands(weight_one, bias_one, weight_two, width):
    hid = weight_one.shape[0]
    pick, grow, _, _ = band_tables(hid)
    blocks = pl.cdiv(width, STEP)
    tail = width - STEP * (blocks - 1)

    def body(pick, grow, w1, w2, bias, band1, band2, bias_full):
        band_kernel(pick, grow, w1, w2, bias, tail, band1, band2, bias_full)

    return pl.pallas_call(
        body,
        out_shape=(
            jax.ShapeDtypeStruct((hid * STEP, 27 * WIN), jnp.bfloat16),
            jax.ShapeDtypeStruct((2, 27 * WIN, hid * STEP), jnp.bfloat16),
            jax.ShapeDtypeStruct((hid * STEP, 128), jnp.float32),
        ),
        in_specs=[pl.BlockSpec(memory_space=VMEM)] * 5,
        out_specs=(pl.BlockSpec(memory_space=VMEM),) * 3,
        name="bands",
    )(
        jnp.asarray(pick, jnp.bfloat16),
        jnp.asarray(grow, jnp.bfloat16),
        weight_one,
        weight_two,
        jnp.broadcast_to(bias_one[:, None], (hid, 128)),
    )


def shifted(values, by):
    lane = lax.broadcasted_iota(jnp.int32, values.shape, values.ndim - 1)
    width = values.shape[-1]
    if by == 1:
        return jnp.where(lane == 0, 0.0, pltpu.roll(values, 1, values.ndim - 1))
    return jnp.where(lane == width - 1, 0.0, pltpu.roll(values, width - 1, values.ndim - 1))


def conv_kernel(rows_a, rows_b, valid, choose, merge, before, own, after, band1, band2, bias1, bias2, out, windows, parts):
    blocks = windows.shape[0]
    width = own.shape[-1]
    ext_i, ext_k = rows_a + 4, rows_b + 4
    hid_i, hid_k = rows_a + 2, rows_b + 2
    pairs = hid_k // 2
    groups = ((before, 0), (own, 2), (after, 2 + rows_a))

    def build(k, carry):
        for ref, at in groups:
            count = rows_a if ref is own else 2
            first = rows_a - 2 if ref is before else 0
            for i in range(count):
                tall = jnp.dot(choose[...], ref[k, first + i], preferred_element_type=jnp.float32)
                for d, piece in enumerate((shifted(tall, 1), tall, shifted(tall, -1))):
                    windows[:, at + i, k, d] = piece.astype(jnp.bfloat16).reshape(blocks, WIN, width)
        return carry

    lax.fori_loop(0, ext_k, build, 0)

    def block_step(block, carry):
        last = (block == blocks - 1).astype(jnp.int32)
        sums = {}
        for i in range(hid_i):
            taps_a = [a for a in range(3) if 1 <= i - a + 1 <= rows_a]
            for p in range(pairs):
                k = 2 * p
                columns = jnp.concatenate(
                    [
                        jnp.concatenate(
                            [
                                windows[block, i + a, k + h : k + h + 3].reshape(9 * WIN, width)
                                for a in range(3)
                            ],
                            axis=0,
                        )
                        for h in range(2)
                    ],
                    axis=1,
                )
                hidden = jnp.dot(band1[...], columns, preferred_element_type=jnp.float32)
                bias = bias1[...]
                hidden = jnp.maximum(hidden + jnp.concatenate([bias, bias], axis=1), 0.0).astype(jnp.bfloat16)
                taps_c = [c for c in range(3) if any(1 <= k + h - c + 1 <= rows_b for h in range(2))]
                size = 3 * WIN
                weights = jnp.concatenate(
                    [band2[last, pl.ds((3 * a + c) * size, size), :] for a in taps_a for c in taps_c], axis=0
                )
                result = jnp.dot(weights, hidden, preferred_element_type=jnp.float32)
                at = 0
                for a in taps_a:
                    for c in taps_c:
                        for d in range(3):
                            for h in range(2):
                                o_i, o_k = i - a, k + h - c
                                if 0 <= o_k < rows_b:
                                    piece = result[at : at + WIN, h * width : (h + 1) * width]
                                    if i in (0, hid_i - 1) or k + h in (0, hid_k - 1):
                                        piece = piece * (valid[0, i] * valid[1, k + h])
                                    key = (o_i, o_k, d)
                                    sums[key] = sums[key] + piece if key in sums else piece
                            at += WIN
        for o_i in range(rows_a):
            for o_k in range(rows_b):
                parts[o_i, o_k, pl.ds(pl.multiple_of(block * WIN, WIN), WIN), :] = (
                    shifted(sums[o_i, o_k, 0], 1) + sums[o_i, o_k, 1] + shifted(sums[o_i, o_k, 2], -1)
                )
        return carry

    lax.fori_loop(0, blocks, block_step, 0)
    for o_i in range(rows_a):
        for o_k in range(rows_b):
            joined = jnp.dot(
                merge[...], parts[o_i, o_k], precision=lax.Precision.HIGHEST, preferred_element_type=jnp.float32
            )
            out[o_i, :, o_k, :] = jnp.maximum(joined + bias2[0], 0.0)


def convolve(valid, before, own, after, band1, band2, bias_full, bias_two):
    ext_k, rows_a, width, _ = own.shape
    rows_b = ext_k - 4
    blocks = band_blocks = pl.cdiv(width, STEP)
    choose = np.zeros((blocks * WIN, width), np.float32)
    merge = np.zeros((width, blocks * WIN), np.float32)
    for block in range(blocks):
        for w in range(WIN):
            j = STEP * block - 1 + w
            if 0 <= j < width:
                choose[block * WIN + w, j] = 1.0
                merge[j, block * WIN + w] = 1.0
    return pl.pallas_call(
        functools.partial(conv_kernel, rows_a, rows_b),
        out_shape=jax.ShapeDtypeStruct((rows_a, width, rows_b, own.shape[-1]), jnp.float32),
        in_specs=[pl.BlockSpec(memory_space=SMEM)]
        + [pl.BlockSpec(memory_space=VMEM)] * 8
        + [pl.BlockSpec(memory_space=SMEM)],
        out_specs=pl.BlockSpec(memory_space=VMEM),
        scratch_shapes=[
            VMEM((blocks, rows_a + 4, ext_k, 3, WIN, own.shape[-1]), jnp.bfloat16),
            VMEM((rows_a, rows_b, blocks * WIN, own.shape[-1]), jnp.float32),
        ],
        name="convolve",
    )(
        valid,
        jnp.asarray(choose, jnp.bfloat16),
        jnp.asarray(merge, jnp.float32),
        before,
        own,
        after,
        band1,
        band2,
        bias_full,
        bias_two,
    )


def per_device(features_a, features_b, weight_one, bias_one, weight_two, bias_two):
    at_a, at_b = lax.axis_index("ra"), lax.axis_index("rb")
    n_a, n_b = lax.axis_size("ra"), lax.axis_size("rb")
    rows_a, rows_b = features_a.shape[0], features_b.shape[0]
    place = jnp.stack([at_a, at_b]).astype(jnp.int32)
    blocks_a = spread(features_a, "rb")
    blocks_b = spread(features_b, "ra")
    corr = correlate(place, blocks_a, blocks_b)
    band1, band2, bias_full = bands(weight_one, bias_one, weight_two, corr.shape[2])
    below, above = halo(corr, "rb")
    own = jnp.concatenate([below[rows_b - 2 :], corr, above[:2]], axis=0)
    before, after = halo(own, "ra")

    def inside(at, count, rows):
        ext = jnp.arange(rows + 2)
        where = at * rows + ext - 1
        return ((where >= 0) & (where < count * rows)).astype(jnp.float32)

    valid = jnp.zeros((2, 8), jnp.float32)
    valid = valid.at[0, : rows_a + 2].set(inside(at_a, n_a, rows_a))
    valid = valid.at[1, : rows_b + 2].set(inside(at_b, n_b, rows_b))
    return convolve(valid, before, own, after, band1, band2, bias_full, bias_two)


def solution(mesh):
    return jax.shard_map(
        per_device,
        mesh=mesh,
        in_specs=(P("ra", "rb", None), P("rb", "ra", None), P(), P(), P(), P()),
        out_specs=P("ra", None, "rb", None),
        check_vma=False,
    )
```

```python
import functools

import jax
import jax.numpy as jnp
import numpy as np
from jax import lax
from jax.experimental import pallas as pl
from jax.experimental.pallas import tpu as pltpu
from jax.sharding import PartitionSpec as P


WIN = 16
STEP = WIN - 2
VMEM = pltpu.VMEM
SMEM = pltpu.SMEM


def swap(block, axis, mask):
    count = lax.axis_size(axis)
    return lax.ppermute(block, axis, [(i, i ^ mask) for i in range(count)])


def neighbours(block, axis):
    count = lax.axis_size(axis)
    across = [(i, i + 1) for i in range(1, count - 1, 2)]
    far = lax.ppermute(block, axis, across + [(j, i) for i, j in across])
    return swap(block, axis, 1), far


def gathered(block, axis):
    count = lax.axis_size(axis)
    even = jnp.stack([block] + [swap(block, axis, mask) for mask in range(2, count, 2)])
    return even, swap(even, axis, 1)


def normalize(values):
    values = values.astype(jnp.float32)
    scale = lax.rsqrt(jnp.sum(values * values, axis=-1, keepdims=True) + 1e-06)
    return (values * scale).astype(jnp.bfloat16)


def corr_kernel(a_even, a_odd, b_even, b_odd, out, all_a, all_b):
    at_a, at_b = lax.axis_index("ra"), lax.axis_index("rb")
    odd = at_b & 1
    rows_b = b_even.shape[2]
    ext = all_b.shape[0]
    near_from = (1 - odd) * (ext - 2)
    far_from = odd * (ext - 2)
    for low, ref in enumerate((a_even, a_odd)):
        cols = ref.shape[2]
        for m in range(ref.shape[0]):
            source = at_b ^ (2 * m + low)
            start = pl.multiple_of(source * cols, cols)
            all_a[:, pl.ds(start, cols), :] = normalize(ref[m]).astype(all_a.dtype)
    for low, ref in enumerate((b_even, b_odd)):
        cols = ref.shape[3]
        for m in range(ref.shape[0]):
            source = at_a ^ (2 * m + low)
            start = pl.multiple_of(source * cols, cols)
            for k in range(rows_b):
                all_b[2 + k, pl.ds(start, cols), :] = normalize(ref[m, 0, k]).astype(all_b.dtype)
            for side, begin, skip in ((1, near_from, odd), (2, far_from, 1 - odd)):
                for k in range(2):
                    row = ref[m, side, skip * (rows_b - 2) + k]
                    all_b[begin + k, pl.ds(start, cols), :] = normalize(row).astype(all_b.dtype)
    for k in range(ext):
        row_b = all_b[k].astype(jnp.bfloat16)
        for i in range(out.shape[1]):
            out[k, i] = lax.dot_general(
                all_a[i].astype(jnp.bfloat16),
                row_b,
                (((1,), (1,)), ((), ())),
                preferred_element_type=jnp.float32,
            ).astype(jnp.bfloat16)


def correlate(a_even, a_odd, b_even, b_odd):
    half_a, rows_a, cols_a, channels = a_even.shape
    half_b, _, rows_b, cols_b, _ = b_even.shape
    wide_a, wide_b = 2 * half_a * cols_a, 2 * half_b * cols_b
    kind_a = jnp.bfloat16 if cols_a % 16 == 0 else jnp.float32
    kind_b = jnp.bfloat16 if cols_b % 16 == 0 else jnp.float32
    return pl.pallas_call(
        corr_kernel,
        out_shape=jax.ShapeDtypeStruct((rows_b + 4, rows_a, wide_a, wide_b), jnp.bfloat16),
        in_specs=[pl.BlockSpec(memory_space=VMEM)] * 4,
        out_specs=pl.BlockSpec(memory_space=VMEM),
        scratch_shapes=[
            VMEM((rows_a, wide_a, channels), kind_a),
            VMEM((rows_b + 4, wide_b, channels), kind_b),
        ],
        name="correlate",
    )(a_even, a_odd, b_even, b_odd)


def band_tables(hid):
    taps = np.arange(81)
    ta, tb, tc, td = taps // 27, taps // 9 % 3, taps // 3 % 3, taps % 3
    col = np.arange(27 * WIN)
    ca, cc, cd, cw = col // (9 * WIN), col // (3 * WIN) % 3, col // WIN % 3, col % WIN
    pick = np.zeros((3, 81, 27 * WIN), np.float32)
    for b in range(3):
        pick[b] = (
            (tb[:, None] == b)
            & (ta[:, None] == ca[None])
            & (tc[:, None] == cc[None])
            & (td[:, None] == cd[None])
        )
    row = np.arange(hid * STEP)
    ro, rj = row // STEP, row % STEP
    grow = (ro[:, None] == np.arange(hid)[None]).astype(np.float32)
    return pick, grow, cw, rj


def band_kernel(pick, grow, w1, w2, bias, tail, band1, band2, bias_full):
    rows, cols = band1.shape
    jj = lax.broadcasted_iota(jnp.int32, (rows, cols), 0) % STEP
    ww = lax.broadcasted_iota(jnp.int32, (rows, cols), 1) % WIN
    total = jnp.zeros((rows, cols), jnp.float32)
    for b in range(3):
        wide = jnp.dot(w1[...], pick[b], preferred_element_type=jnp.float32).astype(jnp.bfloat16)
        tall = jnp.dot(grow[...], wide, preferred_element_type=jnp.float32)
        total = total + jnp.where(ww - jj == b, tall, 0.0)
    band1[...] = total.astype(jnp.bfloat16)
    jj = lax.broadcasted_iota(jnp.int32, (cols, rows), 1) % STEP
    rr = lax.broadcasted_iota(jnp.int32, (cols, rows), 0) % WIN
    total = jnp.zeros((cols, rows), jnp.float32)
    for b in range(3):
        wide = lax.dot_general(
            pick[b], w2[...], (((0,), (1,)), ((), ())), preferred_element_type=jnp.float32
        ).astype(jnp.bfloat16)
        tall = lax.dot_general(
            wide, grow[...], (((1,), (1,)), ((), ())), preferred_element_type=jnp.float32
        )
        total = total + jnp.where(jj - rr + 2 == b, tall, 0.0)
    band2[0] = total.astype(jnp.bfloat16)
    band2[1] = jnp.where(jj < tail, total, 0.0).astype(jnp.bfloat16)
    bias_full[...] = jnp.broadcast_to(
        lax.dot_general(
            grow[...].astype(jnp.float32),
            bias[...],
            (((1,), (0,)), ((), ())),
            precision=lax.Precision.HIGHEST,
            preferred_element_type=jnp.float32,
        ),
        bias_full.shape,
    )


def bands(weight_one, bias_one, weight_two, width):
    hid = weight_one.shape[0]
    pick, grow, _, _ = band_tables(hid)
    blocks = pl.cdiv(width, STEP)
    tail = width - STEP * (blocks - 1)

    def body(pick, grow, w1, w2, bias, band1, band2, bias_full):
        band_kernel(pick, grow, w1, w2, bias, tail, band1, band2, bias_full)

    return pl.pallas_call(
        body,
        out_shape=(
            jax.ShapeDtypeStruct((hid * STEP, 27 * WIN), jnp.bfloat16),
            jax.ShapeDtypeStruct((2, 27 * WIN, hid * STEP), jnp.bfloat16),
            jax.ShapeDtypeStruct((hid * STEP, 128), jnp.float32),
        ),
        in_specs=[pl.BlockSpec(memory_space=VMEM)] * 5,
        out_specs=(pl.BlockSpec(memory_space=VMEM),) * 3,
        name="bands",
    )(
        jnp.asarray(pick, jnp.bfloat16),
        jnp.asarray(grow, jnp.bfloat16),
        weight_one,
        weight_two,
        jnp.broadcast_to(bias_one[:, None], (hid, 128)),
    )


def shifted(values, by):
    lane = lax.broadcasted_iota(jnp.int32, values.shape, values.ndim - 1)
    width = values.shape[-1]
    if by == 1:
        return jnp.where(lane == 0, 0.0, pltpu.roll(values, 1, values.ndim - 1))
    return jnp.where(lane == width - 1, 0.0, pltpu.roll(values, width - 1, values.ndim - 1))


def conv_kernel(n_a, n_b, own, near, far, band1, band2, bias1, bias2, out, stage, window_a, window_b, total):
    ext_k, rows_a, width, lanes = own.shape
    rows_b = ext_k - 4
    hid_i, hid_k = rows_a + 2, rows_b + 2
    pairs = hid_k // 2
    blocks = pl.cdiv(width, STEP)
    at_a, at_b = lax.axis_index("ra"), lax.axis_index("rb")
    odd = at_a & 1

    def inside(at, count, rows, row):
        where = at * rows + row - 1
        return ((where >= 0) & (where < count * rows)).astype(jnp.float32)

    valid_i = [inside(at_a, n_a, rows_a, i) for i in range(hid_i)]
    valid_k = [inside(at_b, n_b, rows_b, k) for k in range(hid_k)]
    total[...] = jnp.zeros_like(total)

    def fill(k, carry):
        for i in range(rows_a + 4):
            stage[i, k, 0:8, :] = jnp.zeros((8, lanes), jnp.float32)
            stage[i, k, 8 + width :, :] = jnp.zeros((stage.shape[2] - 8 - width, lanes), jnp.float32)
        for i in range(rows_a):
            stage[2 + i, k, 8 : 8 + width, :] = own[k, i].astype(jnp.float32)
        for i in range(2):
            row = near[k, odd * (rows_a - 2) + i]
            stage[(1 - odd) * (rows_a + 2) + i, k, 8 : 8 + width, :] = row.astype(jnp.float32)
            row = far[k, (1 - odd) * (rows_a - 2) + i]
            stage[odd * (rows_a + 2) + i, k, 8 : 8 + width, :] = row.astype(jnp.float32)
        return carry

    lax.fori_loop(0, ext_k, fill, 0)

    def build(block, window, rows):
        for i in rows:
            for k in range(ext_k):
                tall = stage[i, k, pl.ds(STEP * block + 7, WIN), :]
                for d, piece in enumerate((shifted(tall, 1), tall, shifted(tall, -1))):
                    window[i, k, d] = piece.astype(jnp.bfloat16)

    def convolve_block(block, window, following):
        last = (block == blocks - 1).astype(jnp.int32)
        sums = {}

        def first(i):
            columns = jnp.concatenate(
                [
                    jnp.concatenate(
                        [window[i + a, k : k + 3].reshape(9 * WIN, lanes) for a in range(3)], axis=0
                    )
                    for k in range(hid_k)
                ],
                axis=1,
            )
            hidden = jnp.dot(band1[...], columns, preferred_element_type=jnp.float32)
            bias = bias1[...]
            return jnp.maximum(hidden + jnp.concatenate([bias] * hid_k, axis=1), 0.0).astype(jnp.bfloat16)

        def second(i, hidden):
            taps_a = [a for a in range(3) if 1 <= i - a + 1 <= rows_a]
            for p in range(pairs):
                k = 2 * p
                taps_c = [c for c in range(3) if any(1 <= k + h - c + 1 <= rows_b for h in range(2))]
                size = 3 * WIN
                weights = jnp.concatenate(
                    [band2[last, pl.ds((3 * a + c) * size, size), :] for a in taps_a for c in taps_c], axis=0
                )
                result = jnp.dot(
                    weights, hidden[:, k * lanes : (k + 2) * lanes], preferred_element_type=jnp.float32
                )
                at = 0
                for a in taps_a:
                    for c in taps_c:
                        for d in range(3):
                            for h in range(2):
                                o_i, o_k = i - a, k + h - c
                                if 0 <= o_k < rows_b:
                                    piece = result[at : at + WIN, h * lanes : (h + 1) * lanes]
                                    if i in (0, hid_i - 1) or k + h in (0, hid_k - 1):
                                        piece = piece * (valid_i[i] * valid_k[k + h])
                                    key = (o_i, o_k, d)
                                    sums[key] = sums[key] + piece if key in sums else piece
                            at += WIN

        ext_i = rows_a + 4
        held = first(0)
        following(range(0, ext_i // hid_i + 1))
        for i in range(1, hid_i):
            fresh = first(i)
            second(i - 1, held)
            following(range(ext_i * i // hid_i + 1, ext_i * (i + 1) // hid_i + 1) if i < hid_i - 1 else range(ext_i * i // hid_i + 1, ext_i))
            held = fresh
        second(hid_i - 1, held)
        for o_i in range(rows_a):
            for o_k in range(rows_b):
                rows = pl.ds(STEP * block + 7, WIN)
                total[o_i, o_k, rows, :] = total[o_i, o_k, rows, :] + (
                    shifted(sums[o_i, o_k, 0], 1) + sums[o_i, o_k, 1] + shifted(sums[o_i, o_k, 2], -1)
                )

    build(0, window_a, range(rows_a + 4))

    def two(step, carry):
        block = 2 * step
        convolve_block(block, window_a, lambda rows: build(block + 1, window_b, rows))
        convolve_block(block + 1, window_b, lambda rows: build(block + 2, window_a, rows))
        return carry

    lax.fori_loop(0, blocks // 2, two, 0)
    for o_i in range(rows_a):
        for o_k in range(rows_b):
            out[o_i, :, o_k, :] = jnp.maximum(total[o_i, o_k, 8 : 8 + width, :] + bias2[0], 0.0)


def convolve(n_a, n_b, own, near, far, band1, band2, bias_full, bias_two):
    ext_k, rows_a, width, lanes = own.shape
    rows_b = ext_k - 4
    blocks = pl.cdiv(width, STEP)
    assert blocks % 2 == 0
    tall = pl.cdiv(STEP * blocks + 7 + WIN, 8) * 8
    window = VMEM((rows_a + 4, ext_k, 3, WIN, lanes), jnp.bfloat16)
    return pl.pallas_call(
        functools.partial(conv_kernel, n_a, n_b),
        out_shape=jax.ShapeDtypeStruct((rows_a, width, rows_b, lanes), jnp.float32),
        in_specs=[pl.BlockSpec(memory_space=VMEM)] * 6 + [pl.BlockSpec(memory_space=SMEM)],
        out_specs=pl.BlockSpec(memory_space=VMEM),
        scratch_shapes=[
            VMEM((rows_a + 4, ext_k, tall, lanes), jnp.float32),
            window,
            window,
            VMEM((rows_a, rows_b, tall, lanes), jnp.float32),
        ],
        name="convolve",
    )(own, near, far, band1, band2, bias_full, bias_two)


def per_device(features_a, features_b, weight_one, bias_one, weight_two, bias_two):
    near_b, far_b = neighbours(features_b, "rb")
    a_even, a_odd = gathered(features_a, "rb")
    b_even, b_odd = gathered(jnp.stack([features_b, near_b, far_b]), "ra")
    tables = bands(weight_one, bias_one, weight_two, 2 * a_even.shape[0] * a_even.shape[2])
    own = correlate(a_even, a_odd, b_even, b_odd)
    near, far = neighbours(own, "ra")
    return convolve(lax.axis_size("ra"), lax.axis_size("rb"), own, near, far, *tables, bias_two)


def solution(mesh):
    return jax.shard_map(
        per_device,
        mesh=mesh,
        in_specs=(P("ra", "rb", None), P("rb", "ra", None), P(), P(), P(), P()),
        out_specs=P("ra", None, "rb", None),
        check_vma=False,
    )
```

```python
import functools

import jax
import jax.numpy as jnp
import numpy as np
from jax import lax
from jax.experimental import pallas as pl
from jax.experimental.pallas import tpu as pltpu
from jax.sharding import PartitionSpec as P


WIN = 16
STEP = WIN - 2
VMEM = pltpu.VMEM
SMEM = pltpu.SMEM


def resident(*arrays):
    return [pltpu.with_memory_space_constraint(x, VMEM) for x in arrays]


def swap(block, axis, mask):
    count = lax.axis_size(axis)
    return lax.ppermute(block, axis, [(i, i ^ mask) for i in range(count)])


def neighbours(block, axis):
    count = lax.axis_size(axis)
    across = [(i, i + 1) for i in range(1, count - 1, 2)]
    far = lax.ppermute(block, axis, across + [(j, i) for i, j in across])
    return swap(block, axis, 1), far


def gathered(block, axis):
    count = lax.axis_size(axis)
    even = jnp.stack([block] + [swap(block, axis, mask) for mask in range(2, count, 2)])
    return even, swap(even, axis, 1)


def normalize(values):
    values = values.astype(jnp.float32)
    scale = lax.rsqrt(jnp.sum(values * values, axis=-1, keepdims=True) + 1e-06)
    return (values * scale).astype(jnp.bfloat16)


def corr_kernel(a_even, a_odd, b_even, b_odd, out, all_a, all_b):
    at_a, at_b = lax.axis_index("ra"), lax.axis_index("rb")
    odd = at_b & 1
    rows_b = b_even.shape[2]
    ext = all_b.shape[0]
    begins = (2, (1 - odd) * (ext - 2), odd * (ext - 2))
    skips = (0, odd * (rows_b - 2), (1 - odd) * (rows_b - 2))
    for low, (a_in, b_in) in enumerate(((a_even, b_even), (a_odd, b_odd))):
        cols = a_in.shape[2]
        for m in range(a_in.shape[0]):
            source = at_b ^ (2 * m + low)
            start = pl.multiple_of(source * cols, cols)
            all_a[:, pl.ds(start, cols), :] = normalize(a_in[m]).astype(all_a.dtype)
        cols = b_in.shape[3]
        for m in range(b_in.shape[0]):
            source = at_a ^ (2 * m + low)
            start = pl.multiple_of(source * cols, cols)
            for side in range(3):
                for k in range(2 if side else rows_b):
                    row = b_in[m, side, skips[side] + k]
                    all_b[begins[side] + k, pl.ds(start, cols), :] = normalize(row).astype(all_b.dtype)
    rows_a, wide_a, channels = all_a.shape
    wide_b = all_b.shape[1]
    flat_a = all_a[...].astype(jnp.bfloat16).reshape(rows_a * wide_a, channels)
    for k in range(0, ext, 2):
        product = lax.dot_general(
            flat_a,
            all_b[k : k + 2].astype(jnp.bfloat16).reshape(2 * wide_b, channels),
            (((1,), (1,)), ((), ())),
            preferred_element_type=jnp.float32,
        ).astype(jnp.bfloat16)
        for h in range(2):
            for i in range(rows_a):
                out[k + h, i] = product[i * wide_a : (i + 1) * wide_a, h * wide_b : (h + 1) * wide_b]


def correlate(a_even, a_odd, b_even, b_odd):
    half_a, rows_a, cols_a, channels = a_even.shape
    half_b, _, rows_b, cols_b, _ = b_even.shape
    wide_a, wide_b = 2 * half_a * cols_a, 2 * half_b * cols_b
    kind_a = jnp.bfloat16 if cols_a % 16 == 0 else jnp.float32
    kind_b = jnp.bfloat16 if cols_b % 16 == 0 else jnp.float32
    return pl.pallas_call(
        corr_kernel,
        out_shape=VMEM((rows_b + 4, rows_a, wide_a, wide_b), jnp.bfloat16),
        in_specs=[pl.BlockSpec(memory_space=VMEM)] * 4,
        out_specs=pl.BlockSpec(memory_space=VMEM),
        scratch_shapes=[
            VMEM((rows_a, wide_a, channels), kind_a),
            VMEM((rows_b + 4, wide_b, channels), kind_b),
        ],
        name="correlate",
    )(*resident(a_even, a_odd, b_even, b_odd))


def band_tables(hid):
    taps = np.arange(81)[:, None]
    col = np.arange(27 * WIN)[None]
    pick = np.zeros((2, 3, 81, 27 * WIN), np.float32)
    for p in range(2):
        along = col // (9 * WIN) if p else 2 - col // (9 * WIN)
        same = (taps // 27 == along) & (taps // 3 % 3 == col // (3 * WIN) % 3) & (taps % 3 == col // WIN % 3)
        for b in range(3):
            pick[p, b] = same & (taps // 9 % 3 == b)
    grow = np.arange(hid * STEP)[:, None] // STEP == np.arange(hid)[None]
    return pick, grow.astype(np.float32)


def band_kernel(tail, pick, grow, w1, w2, bias, band1, band2, bias_full):
    odd = lax.axis_index("ra") & 1
    rows, cols = band1.shape
    hid = w1.shape[0]

    def masked(parts, jj, ww):
        reach = ww - jj
        total = jnp.where(reach == 0, parts[0], 0.0)
        for b in (1, 2):
            total = total + jnp.where(reach == b, parts[b], 0.0)
        return total

    column = lax.broadcasted_iota(jnp.int32, (rows, 1), 0)
    group = sum((column >= STEP * o).astype(jnp.int32) for o in range(1, hid))
    parts = [
        jnp.dot(
            grow[...],
            jnp.dot(w1[...], pick[odd, b], preferred_element_type=jnp.float32).astype(jnp.bfloat16),
            preferred_element_type=jnp.float32,
        )
        for b in range(3)
    ]
    across = lax.broadcasted_iota(jnp.int32, (1, cols), 1) & (WIN - 1)
    band1[...] = masked(parts, column - STEP * group, across).astype(jnp.bfloat16)
    total = jnp.zeros(bias_full.shape, jnp.float32)
    for o in range(hid):
        total = jnp.where(group == o, bias[o], total)
    bias_full[...] = total

    row = lax.broadcasted_iota(jnp.int32, (1, rows), 1)
    jj = row - STEP * sum((row >= STEP * o).astype(jnp.int32) for o in range(1, hid))
    rr = lax.broadcasted_iota(jnp.int32, (cols, 1), 0) & (WIN - 1)
    parts = [
        lax.dot_general(
            lax.dot_general(
                pick[odd, b], w2[...], (((0,), (1,)), ((), ())), preferred_element_type=jnp.float32
            ).astype(jnp.bfloat16),
            grow[...],
            (((1,), (1,)), ((), ())),
            preferred_element_type=jnp.float32,
        )
        for b in range(3)
    ]
    total = masked(parts, rr - 2, jj)
    band2[0] = total.astype(jnp.bfloat16)
    band2[1] = jnp.where(jj < tail, total, 0.0).astype(jnp.bfloat16)


def bands(weight_one, bias_one, weight_two, width):
    hid = weight_one.shape[0]
    pick, grow = band_tables(hid)
    blocks = pl.cdiv(width, STEP)
    return pl.pallas_call(
        functools.partial(band_kernel, width - STEP * (blocks - 1)),
        out_shape=(
            VMEM((hid * STEP, 27 * WIN), jnp.bfloat16),
            VMEM((2, 27 * WIN, hid * STEP), jnp.bfloat16),
            VMEM((hid * STEP, 128), jnp.float32),
        ),
        in_specs=[pl.BlockSpec(memory_space=VMEM)] * 4 + [pl.BlockSpec(memory_space=SMEM)],
        out_specs=(pl.BlockSpec(memory_space=VMEM),) * 3,
        name="bands",
    )(jnp.asarray(pick, jnp.bfloat16), jnp.asarray(grow, jnp.bfloat16), weight_one, weight_two, bias_one)


def shifted(values, by):
    lane = lax.broadcasted_iota(jnp.int32, values.shape, values.ndim - 1)
    width = values.shape[-1]
    if by == 1:
        return jnp.where(lane == 0, 0.0, pltpu.roll(values, 1, values.ndim - 1))
    return jnp.where(lane == width - 1, 0.0, pltpu.roll(values, width - 1, values.ndim - 1))


def conv_kernel(part, unroll, n_a, n_b, *refs):
    refs = list(refs)
    own, side, band1, band2, bias1 = refs[:5]
    before, bias2 = refs[5:7] if part else (None, None)
    out, stage = refs[5 + 2 * part : 7 + 2 * part]
    total = refs[7 + 2 * part] if part else out
    windows = refs[7 + 3 * part :]
    ext_k, rows_a, width, lanes = own.shape
    rows_b = ext_k - 4
    hid_i, hid_k = rows_a + 2, rows_b + 2
    pairs = hid_k // 2
    blocks = pl.cdiv(width, STEP)
    at_a, at_b = lax.axis_index("ra"), lax.axis_index("rb")
    odd = at_a & 1

    def inside(at, count, rows, row):
        where = at * rows + row - 1
        return ((where >= 0) & (where < count * rows)).astype(jnp.float32)

    def actual(row, rows):
        return odd * row + (1 - odd) * (rows - 1 - row)

    valid_i = [inside(at_a, n_a, rows_a, actual(i, hid_i)) for i in range(hid_i)]
    valid_k = [inside(at_b, n_b, rows_b, k) for k in range(hid_k)]
    total[...] = before[...] if part else jnp.zeros_like(total)
    tall = stage.shape[2]

    def fill(k, carry):
        for i in range(4):
            stage[i, k, 0:8, :] = jnp.zeros((8, lanes), jnp.float32)
            stage[i, k, 8 + width :, :] = jnp.zeros((tall - 8 - width, lanes), jnp.float32)
        for ref, first in ((own, 0 if part else 2), (side, 2 if part else 0)):
            for i in range(2):
                stage[first + i, k, 8 : 8 + width, :] = ref[k, actual(i, rows_a)].astype(jnp.float32)
        return carry

    lax.fori_loop(0, ext_k, fill, 0)

    def build(block, window, rows):
        for i in rows:
            for k in range(ext_k):
                piece = stage[i, k, pl.ds(STEP * block + 7, WIN), :]
                for d, moved in enumerate((shifted(piece, 1), piece, shifted(piece, -1))):
                    window[i, k, d] = moved.astype(jnp.bfloat16)

    def first(i, window):
        columns = jnp.concatenate(
            [
                jnp.concatenate([window[i + a, k : k + 3].reshape(9 * WIN, lanes) for a in range(3)], axis=0)
                for k in range(hid_k)
            ],
            axis=1,
        )
        hidden = jnp.dot(band1[...], columns, preferred_element_type=jnp.float32)
        bias = bias1[...]
        return jnp.maximum(hidden + jnp.concatenate([bias] * hid_k, axis=1), 0.0).astype(jnp.bfloat16)

    def second(local, hidden, last, sums):
        i = 2 * part + local
        taps_a = [a for a in range(3) if 0 <= i - a < rows_a]
        for p in range(pairs):
            k = 2 * p
            taps_c = [c for c in range(3) if any(0 <= k + h - c < rows_b for h in range(2))]
            size = 3 * WIN
            weights = jnp.concatenate(
                [band2[last, pl.ds((3 * a + c) * size, size), :] for a in taps_a for c in taps_c], axis=0
            )
            result = jnp.dot(weights, hidden[:, k * lanes : (k + 2) * lanes], preferred_element_type=jnp.float32)
            at = 0
            for a in taps_a:
                for c in taps_c:
                    for d in range(3):
                        for h in range(2):
                            o_i, o_k = i - a, k + h - c
                            if 0 <= o_k < rows_b:
                                piece = result[at : at + WIN, h * lanes : (h + 1) * lanes]
                                if i in (0, hid_i - 1) or k + h in (0, hid_k - 1):
                                    piece = piece * (valid_i[i] * valid_k[k + h])
                                key = (o_i, o_k, d)
                                sums[key] = sums[key] + piece if key in sums else piece
                        at += WIN

    def gather(block, sums):
        for o_i in range(rows_a):
            for o_k in range(rows_b):
                rows = pl.ds(STEP * block + 7, WIN)
                total[o_i, o_k, rows, :] = total[o_i, o_k, rows, :] + (
                    shifted(sums[o_i, o_k, 0], 1) + sums[o_i, o_k, 1] + shifted(sums[o_i, o_k, 2], -1)
                )

    build(0, windows[0], range(4))

    def several(step, carry):
        pending = None
        for n in range(unroll):
            block = unroll * step + n
            last = (block == blocks - 1).astype(jnp.int32)
            sums = {}
            following = windows[(n + 1) % unroll]
            for local in range(2):
                hidden = first(local, windows[n])
                if pending is not None:
                    pending()
                build(block + 1, following, range(2 * local, 2 * local + 2))

                def pending(local=local, hidden=hidden, last=last, sums=sums, block=block):
                    second(local, hidden, last, sums)
                    if local == 1:
                        gather(block, sums)

        pending()
        return carry

    lax.fori_loop(0, blocks // unroll, several, 0)
    if part:
        for o_i in range(rows_a):
            for o_k in range(rows_b):
                out[actual(o_i, rows_a), :, o_k, :] = jnp.maximum(
                    total[o_i, o_k, 8 : 8 + width, :] + bias2[0], 0.0
                )


def convolve(part, n_a, n_b, own, side, tables, before=None, bias_two=None):
    ext_k, rows_a, width, lanes = own.shape
    rows_b = ext_k - 4
    blocks = pl.cdiv(width, STEP)
    unroll = 10
    assert rows_a == 2 and rows_b % 2 == 0 and blocks % unroll == 0
    tall = pl.cdiv(STEP * blocks + 7 + WIN, 8) * 8
    sums = (rows_a, rows_b, tall, lanes)
    here = pl.BlockSpec(memory_space=VMEM)
    return pl.pallas_call(
        functools.partial(conv_kernel, part, unroll, n_a, n_b),
        out_shape=jax.ShapeDtypeStruct((rows_a, width, rows_b, lanes), jnp.float32) if part else VMEM(sums, jnp.float32),
        in_specs=[here] * 5 + ([here, pl.BlockSpec(memory_space=SMEM)] if part else []),
        out_specs=here,
        scratch_shapes=[
            VMEM((4, ext_k, tall, lanes), jnp.float32),
        ]
        + [VMEM(sums, jnp.float32)] * part
        + [VMEM((4, ext_k, 3, WIN, lanes), jnp.bfloat16)] * unroll,
    )(*resident(own, side, *tables), *((*resident(before), bias_two) if part else ()))


def per_device(features_a, features_b, weight_one, bias_one, weight_two, bias_two):
    near_b, far_b = neighbours(features_b, "rb")
    a_even, a_odd = gathered(features_a, "rb")
    b_even, b_odd = gathered(jnp.stack([features_b, near_b, far_b]), "ra")
    tables = bands(weight_one, bias_one, weight_two, 2 * a_even.shape[0] * a_even.shape[2])
    own = correlate(a_even, a_odd, b_even, b_odd)
    near, far = neighbours(own, "ra")
    sizes = lax.axis_size("ra"), lax.axis_size("rb")
    half = convolve(0, *sizes, own, near, tables)
    return convolve(1, *sizes, own, far, tables, half, bias_two)


def solution(mesh):
    return jax.shard_map(
        per_device,
        mesh=mesh,
        in_specs=(P("ra", "rb", None), P("rb", "ra", None), P(), P(), P(), P()),
        out_specs=P("ra", None, "rb", None),
        check_vma=False,
    )
```

```python
import functools

import jax
import jax.numpy as jnp
import numpy as np
from jax import lax
from jax.experimental import pallas as pl
from jax.experimental.pallas import tpu as pltpu
from jax.sharding import PartitionSpec as P


WIN = 16
STEP = WIN - 2
VMEM = pltpu.VMEM
SMEM = pltpu.SMEM


GRANT = 24 << 20


def resident(*arrays):
    return [pltpu.with_memory_space_constraint(x, VMEM) for x in arrays]


def swap(block, axis, mask):
    count = lax.axis_size(axis)
    return lax.ppermute(block, axis, [(i, i ^ mask) for i in range(count)])


def neighbours(block, axis):
    count = lax.axis_size(axis)
    across = [(i, i + 1) for i in range(1, count - 1, 2)]
    far = lax.ppermute(block, axis, across + [(j, i) for i, j in across])
    return swap(block, axis, 1), far


def pieces(block, axis):
    count = lax.axis_size(axis)
    even = [block] + [swap(block, axis, mask) for mask in range(2, count, 2)]
    odd = [swap(block, axis, 1)]
    odd += [swap(x, axis, 1) for x in even[1:]]
    return [x for pair in zip(even, odd) for x in pair]


def gathered(block, axis):
    count = lax.axis_size(axis)
    even = jnp.stack([swap(block, axis, mask) for mask in range(2, count, 2)])
    partner = swap(block, axis, 1)
    return block[None], partner[None], even, swap(even, axis, 1)


def normalize(values):
    values = values.astype(jnp.float32)
    scale = lax.rsqrt(jnp.sum(values * values, axis=-1, keepdims=True) + 1e-06)
    return (values * scale).astype(jnp.bfloat16)


def corr_kernel(a_own, a_partner, a_even, a_odd, *refs):
    at_a, at_b = lax.axis_index("ra"), lax.axis_index("rb")
    odd = at_b & 1
    out, all_a, all_b = refs[-3:]
    count = (len(refs) - 3) // 2
    own_b, halo_b = refs[:count], refs[count:-3]
    rows_b = own_b[0].shape[0]
    ext = all_b.shape[0]
    begins = (2, (1 - odd) * (ext - 2), odd * (ext - 2))
    skips = (0, odd * (rows_b - 2), (1 - odd) * (rows_b - 2))
    for first, blocks in enumerate((a_own, a_partner, a_even, a_odd)):
        cols = blocks.shape[2]
        for m in range(blocks.shape[0]):
            start = pl.multiple_of((at_b ^ (2 * m + first)) * cols, cols)
            all_a[:, pl.ds(start, cols), :] = normalize(blocks[m]).astype(all_a.dtype)
    for m in range(count):
        cols = own_b[m].shape[1]
        start = pl.multiple_of((at_a ^ m) * cols, cols)
        for side in range(3):
            for k in range(2 if side else rows_b):
                at = skips[side] + k
                row = halo_b[m][side - 1, at] if side else own_b[m][at]
                all_b[begins[side] + k, pl.ds(start, cols), :] = normalize(row).astype(all_b.dtype)
    rows_a, wide_a, channels = all_a.shape
    wide_b = all_b.shape[1]
    flat_a = all_a[...].astype(jnp.bfloat16).reshape(rows_a * wide_a, channels)
    for k in range(0, ext, 2):
        product = lax.dot_general(
            flat_a,
            all_b[k : k + 2].astype(jnp.bfloat16).reshape(2 * wide_b, channels),
            (((1,), (1,)), ((), ())),
            preferred_element_type=jnp.float32,
        ).astype(jnp.bfloat16)
        for h in range(2):
            for i in range(rows_a):
                out[k + h, i] = product[i * wide_a : (i + 1) * wide_a, h * wide_b : (h + 1) * wide_b]


def correlate(parts_a, own_b, halo_b):
    _, rows_a, cols_a, channels = parts_a[0].shape
    rows_b, cols_b, _ = own_b[0].shape
    wide_a, wide_b = sum(x.shape[0] for x in parts_a) * cols_a, len(own_b) * cols_b
    kind_a = jnp.bfloat16 if cols_a % 16 == 0 else jnp.float32
    kind_b = jnp.bfloat16 if cols_b % 16 == 0 else jnp.float32
    return pl.pallas_call(
        corr_kernel,
        out_shape=VMEM((rows_b + 4, rows_a, wide_a, wide_b), jnp.bfloat16),
        in_specs=[pl.BlockSpec(memory_space=VMEM)] * (4 + 2 * len(own_b)),
        out_specs=pl.BlockSpec(memory_space=VMEM),
        scratch_shapes=[
            VMEM((rows_a, wide_a, channels), kind_a),
            VMEM((rows_b + 4, wide_b, channels), kind_b),
        ],
        compiler_params=pltpu.CompilerParams(vmem_limit_bytes=GRANT),
        name="correlate",
    )(*resident(*parts_a, *own_b, *halo_b))


def band_tables(hid):
    taps = np.arange(81)[:, None]
    col = np.arange(27 * WIN)[None]
    pick = np.zeros((2, 3, 81, 27 * WIN), np.float32)
    for p in range(2):
        along = col // (9 * WIN) if p else 2 - col // (9 * WIN)
        same = (taps // 27 == along) & (taps // 3 % 3 == col // (3 * WIN) % 3) & (taps % 3 == col // WIN % 3)
        for b in range(3):
            pick[p, b] = same & (taps // 9 % 3 == b)
    grow = np.arange(hid * STEP)[:, None] // STEP == np.arange(hid)[None]
    return pick, grow.astype(np.float32)


def band_kernel(tail, pick, grow, w1, w2, bias, band1, band2, bias_full):
    odd = lax.axis_index("ra") & 1
    rows, cols = band1.shape
    hid = w1.shape[0]

    def masked(parts, jj, ww):
        reach = ww - jj
        total = jnp.where(reach == 0, parts[0], 0.0)
        for b in (1, 2):
            total = total + jnp.where(reach == b, parts[b], 0.0)
        return total

    column = lax.broadcasted_iota(jnp.int32, (rows, 1), 0)
    group = sum((column >= STEP * o).astype(jnp.int32) for o in range(1, hid))
    parts = [
        jnp.dot(
            grow[...],
            jnp.dot(w1[...], pick[odd, b], preferred_element_type=jnp.float32).astype(jnp.bfloat16),
            preferred_element_type=jnp.float32,
        )
        for b in range(3)
    ]
    across = lax.broadcasted_iota(jnp.int32, (1, cols), 1) & (WIN - 1)
    band1[...] = masked(parts, column - STEP * group, across).astype(jnp.bfloat16)
    total = jnp.zeros(bias_full.shape, jnp.float32)
    for o in range(hid):
        total = jnp.where(group == o, bias[o], total)
    bias_full[...] = total

    row = lax.broadcasted_iota(jnp.int32, (1, rows), 1)
    jj = row - STEP * sum((row >= STEP * o).astype(jnp.int32) for o in range(1, hid))
    rr = lax.broadcasted_iota(jnp.int32, (cols, 1), 0) & (WIN - 1)
    parts = [
        lax.dot_general(
            lax.dot_general(
                pick[odd, b], w2[...], (((0,), (1,)), ((), ())), preferred_element_type=jnp.float32
            ).astype(jnp.bfloat16),
            grow[...],
            (((1,), (1,)), ((), ())),
            preferred_element_type=jnp.float32,
        )
        for b in range(3)
    ]
    total = masked(parts, rr - 2, jj)
    band2[0] = total.astype(jnp.bfloat16)
    band2[1] = jnp.where(jj < tail, total, 0.0).astype(jnp.bfloat16)


def bands(weight_one, bias_one, weight_two, width):
    hid = weight_one.shape[0]
    pick, grow = band_tables(hid)
    blocks = pl.cdiv(width, STEP)
    return pl.pallas_call(
        functools.partial(band_kernel, width - STEP * (blocks - 1)),
        out_shape=(
            VMEM((hid * STEP, 27 * WIN), jnp.bfloat16),
            VMEM((2, 27 * WIN, hid * STEP), jnp.bfloat16),
            VMEM((hid * STEP, 128), jnp.float32),
        ),
        in_specs=[pl.BlockSpec(memory_space=VMEM)] * 4 + [pl.BlockSpec(memory_space=SMEM)],
        out_specs=(pl.BlockSpec(memory_space=VMEM),) * 3,
        compiler_params=pltpu.CompilerParams(vmem_limit_bytes=GRANT),
        name="bands",
    )(jnp.asarray(pick, jnp.bfloat16), jnp.asarray(grow, jnp.bfloat16), weight_one, weight_two, bias_one)


def shifted(values, by):
    lane = lax.broadcasted_iota(jnp.int32, values.shape, values.ndim - 1)
    width = values.shape[-1]
    if by == 1:
        return jnp.where(lane == 0, 0.0, pltpu.roll(values, 1, values.ndim - 1))
    return jnp.where(lane == width - 1, 0.0, pltpu.roll(values, width - 1, values.ndim - 1))


def conv_kernel(part, unroll, n_a, n_b, *refs):
    refs = list(refs)
    own, side, band1, band2, bias1 = refs[:5]
    before, bias2 = refs[5:7] if part else (None, None)
    out, stage = refs[5 + 2 * part : 7 + 2 * part]
    total = refs[7 + 2 * part] if part else out
    windows = refs[7 + 3 * part :]
    ext_k, rows_a, width, lanes = own.shape
    rows_b = ext_k - 4
    hid_i, hid_k = rows_a + 2, rows_b + 2
    pairs = hid_k // 2
    blocks = pl.cdiv(width, STEP)
    at_a, at_b = lax.axis_index("ra"), lax.axis_index("rb")
    odd = at_a & 1

    def inside(at, count, rows, row):
        where = at * rows + row - 1
        return ((where >= 0) & (where < count * rows)).astype(jnp.float32)

    def actual(row, rows):
        return odd * row + (1 - odd) * (rows - 1 - row)

    valid_i = [inside(at_a, n_a, rows_a, actual(i, hid_i)) for i in range(hid_i)]
    valid_k = [inside(at_b, n_b, rows_b, k) for k in range(hid_k)]
    total[...] = before[...] if part else jnp.zeros_like(total)
    tall = stage.shape[2]

    def fill(k, carry):
        for i in range(4):
            stage[i, k, 0:8, :] = jnp.zeros((8, lanes), jnp.float32)
            stage[i, k, 8 + width :, :] = jnp.zeros((tall - 8 - width, lanes), jnp.float32)
        for ref, first in ((own, 0 if part else 2), (side, 2 if part else 0)):
            for i in range(2):
                stage[first + i, k, 8 : 8 + width, :] = ref[k, actual(i, rows_a)].astype(jnp.float32)
        return carry

    lax.fori_loop(0, ext_k, fill, 0)

    def build(block, window, rows):
        for i in rows:
            for k in range(ext_k):
                piece = stage[i, k, pl.ds(STEP * block + 7, WIN), :]
                for d, moved in enumerate((shifted(piece, 1), piece, shifted(piece, -1))):
                    window[i, k, d] = moved.astype(jnp.bfloat16)

    def first(i, window):
        columns = jnp.concatenate(
            [
                jnp.concatenate([window[i + a, k : k + 3].reshape(9 * WIN, lanes) for a in range(3)], axis=0)
                for k in range(hid_k)
            ],
            axis=1,
        )
        hidden = jnp.dot(band1[...], columns, preferred_element_type=jnp.float32)
        bias = bias1[...]
        return jnp.maximum(hidden + jnp.concatenate([bias] * hid_k, axis=1), 0.0).astype(jnp.bfloat16)

    def second(local, hidden, last, sums):
        i = 2 * part + local
        taps_a = [a for a in range(3) if 0 <= i - a < rows_a]
        for p in range(pairs):
            k = 2 * p
            taps_c = [c for c in range(3) if any(0 <= k + h - c < rows_b for h in range(2))]
            size = 3 * WIN
            weights = jnp.concatenate(
                [band2[last, pl.ds((3 * a + c) * size, size), :] for a in taps_a for c in taps_c], axis=0
            )
            result = jnp.dot(weights, hidden[:, k * lanes : (k + 2) * lanes], preferred_element_type=jnp.float32)
            at = 0
            for a in taps_a:
                for c in taps_c:
                    for d in range(3):
                        for h in range(2):
                            o_i, o_k = i - a, k + h - c
                            if 0 <= o_k < rows_b:
                                piece = result[at : at + WIN, h * lanes : (h + 1) * lanes]
                                if i in (0, hid_i - 1) or k + h in (0, hid_k - 1):
                                    piece = piece * (valid_i[i] * valid_k[k + h])
                                key = (o_i, o_k, d)
                                sums[key] = sums[key] + piece if key in sums else piece
                        at += WIN

    def gather(block, sums):
        for o_i in range(rows_a):
            for o_k in range(rows_b):
                rows = pl.ds(STEP * block + 7, WIN)
                total[o_i, o_k, rows, :] = total[o_i, o_k, rows, :] + (
                    shifted(sums[o_i, o_k, 0], 1) + sums[o_i, o_k, 1] + shifted(sums[o_i, o_k, 2], -1)
                )

    build(0, windows[0], range(4))

    def several(step, carry):
        pending = None
        for n in range(unroll):
            block = unroll * step + n
            last = (block == blocks - 1).astype(jnp.int32)
            sums = {}
            following = windows[(n + 1) % unroll]
            for local in range(2):
                hidden = first(local, windows[n])
                if pending is not None:
                    pending()
                build(block + 1, following, range(2 * local, 2 * local + 2))

                def pending(local=local, hidden=hidden, last=last, sums=sums, block=block):
                    second(local, hidden, last, sums)
                    if local == 1:
                        gather(block, sums)

        pending()
        return carry

    lax.fori_loop(0, blocks // unroll, several, 0)
    if part:
        for o_i in range(rows_a):
            for o_k in range(rows_b):
                out[actual(o_i, rows_a), :, o_k, :] = jnp.maximum(
                    total[o_i, o_k, 8 : 8 + width, :] + bias2[0], 0.0
                )


def convolve(part, n_a, n_b, own, side, tables, before=None, bias_two=None):
    ext_k, rows_a, width, lanes = own.shape
    rows_b = ext_k - 4
    blocks = pl.cdiv(width, STEP)
    unroll = 10
    assert rows_a == 2 and rows_b % 2 == 0 and blocks % unroll == 0
    tall = pl.cdiv(STEP * blocks + 7 + WIN, 8) * 8
    sums = (rows_a, rows_b, tall, lanes)
    here = pl.BlockSpec(memory_space=VMEM)
    return pl.pallas_call(
        functools.partial(conv_kernel, part, unroll, n_a, n_b),
        out_shape=jax.ShapeDtypeStruct((rows_a, width, rows_b, lanes), jnp.float32) if part else VMEM(sums, jnp.float32),
        in_specs=[here] * 5 + ([here, pl.BlockSpec(memory_space=SMEM)] if part else []),
        out_specs=here,
        scratch_shapes=[
            VMEM((4, ext_k, tall, lanes), jnp.float32),
        ]
        + [VMEM(sums, jnp.float32)] * part
        + [VMEM((4, ext_k, 3, WIN, lanes), jnp.bfloat16)] * unroll,
        compiler_params=pltpu.CompilerParams(vmem_limit_bytes=GRANT),
    )(*resident(own, side, *tables), *((*resident(before), bias_two) if part else ()))


def per_device(features_a, features_b, weight_one, bias_one, weight_two, bias_two):
    parts_a = gathered(features_a, "rb")
    sides = neighbours(features_b, "rb")
    own_b = pieces(features_b, "ra")
    sides = jnp.stack(sides)
    halo_b = pieces(sides, "ra")
    tables = bands(weight_one, bias_one, weight_two, lax.axis_size("rb") * features_a.shape[1])
    own = correlate(parts_a, own_b, halo_b)
    near, far = neighbours(own, "ra")
    sizes = lax.axis_size("ra"), lax.axis_size("rb")
    half = convolve(0, *sizes, own, near, tables)
    return convolve(1, *sizes, own, far, tables, half, bias_two)


def solution(mesh):
    return jax.shard_map(
        per_device,
        mesh=mesh,
        in_specs=(P("ra", "rb", None), P("rb", "ra", None), P(), P(), P(), P()),
        out_specs=P("ra", None, "rb", None),
        check_vma=False,
    )
```
